256 devices in a mesh: frames: 16 (over y, x), pix: 16 (over z, core).
Axes of the slice: x: 4, y: 4, z: 8, core: 2. Of those that a mesh axis runs over, the one named last changes fastest.
Arguments:
- photon_counts: int32 [16384, 32768], P('frames', 'pix'), may hold values from 1 to 53, as said below
- flat_field: float32 [32768], P('pix'), may hold values from 0.5 to 2
- owner_counts: int32 [16], replicated, may hold values from 512 to 2048, as said below
Outputs:
- diagonal_tiles: float32 [16384, 1024], P(('frames', 'pix'))
- offdiag_tiles: float32 [16384, 1024], P(('frames', 'pix'))
The draws below stay inside these ranges and needn't reach their ends.
Inputs may be any that keep to these rules, and one draw needn't show every extreme that they name: owner_counts[i] is how many of owner i's 2048 slots, the first ones, hold cycle pixels; some owner holds all 2048. `photon_counts`: whole photon counts of each slot in each frame.
All inputs are finite; a program needn't handle non-finite values.
Results may differ from the reference program's by a relative error of at most 0.0003.
Values may be sent and summed in bfloat16 or wider, within the bound.
No kernel may reach another device: no remote copies, remote signals or barrier semaphores. Data moves between devices by JAX's collectives and lax.ppermute only.
A program may use at most 64 MiB of HBM per device.

```python
import math
import jax
import jax.numpy as jnp
from jax import lax

F = 1024
PCAP = 2048
OWNERS = 16
SLOTS = 32768
FRAMES = 16384
N_FRAMES = 16


def draw_owner_counts(key, part):
    first_key = jax.random.fold_in(key, 11)
    second_key = jax.random.fold_in(key, 23)
    values = jax.random.randint(first_key, (OWNERS,), PCAP // 4, PCAP + 1, dtype=jnp.int32)
    chosen = jax.random.randint(second_key, (), 0, OWNERS, dtype=jnp.int32)
    return values.at[chosen].set(PCAP)


def draw_photon_counts(key, part):
    event_key = jax.random.fold_in(key, 101)
    first_key = jax.random.fold_in(key, 103)
    second_key = jax.random.fold_in(key, 107)
    shot_key = jax.random.fold_in(key, 109)
    events = (jax.random.randint(event_key, (FRAMES,), 0, 8, dtype=jnp.int32) == 0).astype(jnp.int32)
    segment = (jnp.cumsum(events) % 256).astype(jnp.int32)
    first_factor = jax.random.randint(first_key, (256, SLOTS), 0, 4, dtype=jnp.int32)
    second_factor = jax.random.randint(second_key, (256, SLOTS), 0, 4, dtype=jnp.int32)
    speckle = first_factor * second_factor
    owner_ids = jnp.arange(SLOTS, dtype=jnp.int32) // PCAP
    sector_rate = 1 + 3 * owner_ids // max(OWNERS - 1, 1)
    shot_noise = jax.random.randint(shot_key, (FRAMES, SLOTS), 0, 5, dtype=jnp.int32)
    return (1 + sector_rate[None, :] * (speckle[segment] + shot_noise)).astype(jnp.int32)


def shard_levels(rng, dims, split, least, largest):
    loudness, own = 1.0, jax.random.fold_in(rng, 6)
    for dim, blocks in split:
        heights = jnp.exp(jax.random.uniform(jax.random.fold_in(own, dim), (blocks,), jnp.float32, least / len(split), largest / len(split)))
        loudness = loudness * jnp.repeat(heights, dims[dim] // blocks).reshape([-1 if axis == dim else 1 for axis in range(len(dims))])
    return loudness


def setup_inputs(seed: int = 0) -> dict:
    seeds = jax.random.split(jax.random.key(seed), 4)
    return {
        "photon_counts": draw_photon_counts(jax.random.fold_in(seeds[3], 71), 0),
        "flat_field": jnp.clip(jnp.exp(math.log(2.0) - 1.3862944 * jax.random.uniform(seeds[1], (SLOTS,), jnp.float32) ** shard_levels(seeds[1], (SLOTS,), ((0, 16),), -0.2, 0.2)), 0.5, 2.0),
        "owner_counts": draw_owner_counts(jax.random.fold_in(seeds[3], 71), 0),
    }


def gram(left, right):
    return lax.dot_general(left, right, (((1,), (1,)), ((), ())), preferred_element_type=jnp.float32)


def reference(photon_counts, flat_field, owner_counts):
    slot_ids = jnp.arange(SLOTS, dtype=jnp.int32)
    limits = owner_counts[slot_ids // PCAP]
    valid = (slot_ids % PCAP < limits).astype(jnp.float32)
    weights = flat_field * valid
    pixel_total = jnp.sum(owner_counts).astype(jnp.float32)
    blocks = photon_counts.reshape(N_FRAMES, F, SLOTS)

    def scale_block(block):
        corrected = block.astype(jnp.float32) * weights[None, :]
        frame_mean = jnp.sum(corrected, axis=1) / pixel_total
        return (corrected / frame_mean[:, None]).astype(jnp.bfloat16)

    scaled = lax.map(scale_block, blocks)

    def tiles(block_index):
        own_block = scaled[block_index]
        earlier = scaled[jnp.maximum(block_index - 1, 0)]
        diagonal = gram(own_block, own_block) / pixel_total
        keep = (block_index > 0).astype(jnp.float32)
        offdiag = gram(own_block, earlier) / pixel_total * keep
        return diagonal, offdiag

    diagonal_all, offdiag_all = lax.map(tiles, jnp.arange(N_FRAMES, dtype=jnp.int32))
    return diagonal_all.reshape(FRAMES, F), offdiag_all.reshape(FRAMES, F)
```

```python
import jax
import jax.numpy as jnp
from jax import lax
from jax.experimental import pallas as pl
from jax.experimental.pallas import tpu as pltpu
from jax.sharding import Mesh, PartitionSpec as P

BLOCKS, RING, CORES = 16, 8, 2
CHUNKS = 2
F32, BF16 = jnp.float32, jnp.bfloat16


def dot_t(left, right):
    return lax.dot_general(left, right, (((1,), (1,)), ((), ())), preferred_element_type=F32)


def full(shape):
    return pl.BlockSpec(shape, lambda *_: (0,) * len(shape))


SMEM = pl.BlockSpec(memory_space=pltpu.SMEM)


def prep_kernel(place, owners, counts, flat, c_out, hi_out, lo_out, parts_out):
    limit = owners[place[0] * CORES + place[1]]
    slots = lax.broadcasted_iota(jnp.int32, flat.shape, 1)
    weight = jnp.where(slots < limit, flat[...], 0.0)
    value = counts[...].astype(F32)
    c_out[...] = value.astype(BF16)
    product = value * (weight * weight)
    hi = product.astype(BF16)
    hi_out[...] = hi
    lo_out[...] = (product - hi.astype(F32)).astype(BF16)
    w1 = weight.astype(BF16)
    r1 = weight - w1.astype(F32)
    w2 = r1.astype(BF16)
    w3 = (r1 - w2.astype(F32)).astype(BF16)
    row = lax.broadcasted_iota(jnp.int32, parts_out.shape, 0)
    shape = parts_out.shape
    parts = jnp.where(
        row == 0,
        jnp.broadcast_to(w1.astype(F32), shape),
        jnp.where(
            row == 1,
            jnp.broadcast_to(w2.astype(F32), shape),
            jnp.where(row == 2, jnp.broadcast_to(w3.astype(F32), shape), 0.0),
        ),
    )
    parts_out[...] = parts.astype(BF16)


def prep(place, owners, counts, flat):
    frames, slots = counts.shape
    rows = 128
    block = pl.BlockSpec((rows, slots), lambda i: (i, 0))
    wide = jax.ShapeDtypeStruct((frames, slots), BF16)
    return pl.pallas_call(
        prep_kernel,
        grid=(frames // rows,),
        in_specs=[SMEM, SMEM, block, full((1, slots))],
        out_specs=[block, block, block, full((8, slots))],
        out_shape=[wide, wide, wide, jax.ShapeDtypeStruct((8, slots), BF16)],
        compiler_params=pltpu.CompilerParams(vmem_limit_bytes=16 << 20),
        cost_estimate=pl.CostEstimate(flops=8 << 20, bytes_accessed=20 << 20, transcendentals=0),
    )(place, owners, counts, flat)


def diag_kernel(place, hi, lo, parts, right, keep, give, total):
    z, core = place[0], place[1]
    total[...] = dot_t(hi[...], right[...]) + dot_t(lo[...], right[...])
    sums = dot_t(parts[...], right[...])
    for dest in range(RING):
        relative = lax.rem(dest - z + RING, RING)
        mine = pl.multiple_of(dest * 128 + core * 64, 64)
        other = pl.multiple_of(dest * 128 + (1 - core) * 64, 64)
        keep[relative, 0:64, :] = total[pl.ds(mine, 64), :]
        give[relative, 0:64, :] = total[pl.ds(other, 64), :]
        keep[dest, 64:72, :] = sums
        give[dest, 64:72, :] = sums


def diag_gram(place, hi, lo, parts, counts):
    frames, slots = hi.shape
    cols = 256
    out = pl.BlockSpec((RING, 72, cols), lambda i: (0, 0, i))
    shape = jax.ShapeDtypeStruct((RING, 72, frames), F32)
    return pl.pallas_call(
        diag_kernel,
        grid=(frames // cols,),
        in_specs=[
            SMEM,
            full((frames, slots)),
            full((frames, slots)),
            full((8, slots)),
            pl.BlockSpec((cols, slots), lambda i: (i, 0)),
        ],
        out_specs=[out, out],
        out_shape=[shape, shape],
        scratch_shapes=[pltpu.VMEM((frames, cols), F32)],
        compiler_params=pltpu.CompilerParams(vmem_limit_bytes=32 << 20),
        cost_estimate=pl.CostEstimate(flops=8 << 30, bytes_accessed=17 << 20, transcendentals=0),
    )(place, hi, lo, parts, counts)


def cross_kernel(place, hi, lo, got, out):
    z, core = place[0], place[1]
    rows = got.shape[0]
    each = rows // RING
    step = pl.program_id(0)

    @pl.when(core == 0)
    def _():
        piece = dot_t(hi[...], got[...]) + dot_t(lo[...], got[...])
        for half in range(2):
            relative = lax.rem(step * 2 + half - z + RING, RING)
            out[relative, :, :] = piece[half * 128 : (half + 1) * 128, :]

    @pl.when(core == 1)
    def _():
        piece = dot_t(got[...], hi[...]) + dot_t(got[...], lo[...])
        wide = rows // 256
        row = pl.multiple_of((step // wide) * each, each)
        col = pl.multiple_of(lax.rem(step, wide) * 256, 256)
        for dest in range(RING):
            relative = lax.rem(dest - z + RING, RING)
            out[relative, pl.ds(row, each), pl.ds(col, 256)] = piece[dest * each : (dest + 1) * each, :]


def cross_gram(place, hi, lo, got):
    frames, slots = hi.shape
    rows = got.shape[0]
    block = pl.BlockSpec((256, slots), lambda i: (i, 0))
    return pl.pallas_call(
        cross_kernel,
        grid=(frames // 256,),
        in_specs=[SMEM, block, block, full((rows, slots))],
        out_specs=full((RING, 128, rows)),
        out_shape=jax.ShapeDtypeStruct((RING, 128, rows), F32),
        compiler_params=pltpu.CompilerParams(vmem_limit_bytes=28 << 20),
        cost_estimate=pl.CostEstimate(flops=(8 << 30) // CHUNKS, bytes_accessed=10 << 20, transcendentals=0),
    )(place, hi, lo, got)


def hop(value, step):
    return lax.ppermute(value, "z", [(i, (i + step) % RING) for i in range(RING)])


def arms(slab, plus):
    minus = RING - 1 - plus
    ahead = slab(plus)
    for s in range(plus - 1, -1, -1):
        ahead = hop(ahead, 1)
        if s:
            ahead = ahead + slab(s)
    behind = slab(RING - minus)
    for s in range(minus - 1, -1, -1):
        behind = hop(behind, -1)
        if s:
            behind = behind + slab(RING - s)
    return slab(0) + ahead + behind


def flat_pairs(pairs):
    return [(a * CORES + b, c * CORES + d) for (a, b), (c, d) in pairs]


def on_device(photon_counts, flat_field, owner_counts):
    core, z = lax.axis_index("core"), lax.axis_index("z")
    place = jnp.stack([z, core]).astype(jnp.int32)
    frames, slots = photon_counts.shape
    rows = frames // CHUNKS
    each = rows // RING

    both_ways = flat_pairs(
        [p for b in range(BLOCKS - 1) for p in (((b, 0), (b + 1, 0)), ((b + 1, 1), (b, 1)))]
    )
    spread = photon_counts.reshape(RING, CHUNKS, each, slots)
    received = []
    for q in range(CHUNKS):
        near = photon_counts[q * rows : (q + 1) * rows]
        far = spread[:, q].reshape(rows, slots)
        sent = jnp.where(core == 0, near, far).astype(BF16)
        received.append(lax.ppermute(sent, ("frames", "core"), both_ways))

    counts, hi, lo, parts = prep(place, owner_counts, photon_counts, flat_field.reshape(1, slots))
    keep, give = diag_gram(place, hi, lo, parts, counts)
    partner = lax.ppermute(give, "core", [(0, 1), (1, 0)])
    own = arms(lambda s: keep[s] + partner[s], 4)
    sums = own[64] + own[65] + own[66]
    sums_before = lax.ppermute(sums, "frames", [(b, b + 1) for b in range(BLOCKS - 1)])

    columns, moved = [], []
    for q in range(CHUNKS):
        slabs = cross_gram(place, hi, lo, received[q])
        done = arms(lambda s: slabs[s], 3 if q % 2 == 0 else 4)
        side = lax.ppermute(done[64:], "core", [(0, 1)])
        columns.append(jnp.where(core == 0, done[:64], side))
        target = q * CORES // CHUNKS
        moved.append(
            lax.ppermute(
                done, ("frames", "core"), flat_pairs([((b, 1), (b + 1, target)) for b in range(BLOCKS - 1)])
            )
        )
    half = CHUNKS // CORES
    rest = [
        (moved[i] + moved[i + half]).reshape(frames // rows, each, rows).transpose(1, 0, 2).reshape(each, frames)
        for i in range(half)
    ]
    cross = jnp.concatenate(columns, axis=1) + jnp.concatenate(rest, axis=0)

    pixels = jnp.sum(owner_counts).astype(F32)
    mine = pixels / lax.dynamic_slice(sums, (z * 128 + core * 64,), (64,))
    earlier = jnp.where(sums_before > 0, 1.0 / jnp.where(sums_before > 0, sums_before, 1.0), 0.0)
    return (
        own[:64] * mine[:, None] * (1.0 / sums)[None, :],
        cross * mine[:, None] * earlier[None, :],
    )


def solution(mesh):
    fine = Mesh(mesh.devices.reshape(BLOCKS, RING, CORES), ("frames", "z", "core"))
    pix = ("z", "core")
    out = P(("frames", "z", "core"), None)
    return jax.shard_map(
        on_device,
        mesh=fine,
        in_specs=(P("frames", pix), P(pix), P()),
        out_specs=(out, out),
        check_vma=False,
    )
```
